256 devices in a mesh: tok: 2 (over y_hi), fin: 32 (over x, z), fout: 4 (over y_lo, core).
Axes of the slice: x: 4, y: 4 (y_hi: 2, y_lo: 2; y = y_hi * 2 + y_lo), z: 8, core: 2. Of those that a mesh axis runs over, the one named last changes fastest.
Arguments:
- activations: float32 [4096, 8192], P('tok', 'fin'), may hold values from -0.09375 to 0.09375
- out_grad: float32 [4096, 8192], P(('tok', 'fin'), 'fout'), may hold values from -6 to 6
- weight: float32 [8192, 8192], P('fin', 'fout'), may hold values from -0.0625 to 0.0625
Outputs:
- in_grad: float32 [4096, 8192], P(('tok', 'fout'), 'fin')
- weight_grad: float32 [8192, 8192], P(('fin', 'tok'), 'fout')
The draws below stay inside these ranges and needn't reach their ends.
All inputs are finite; a program needn't handle non-finite values.
Results may differ from the reference program's by a relative error of at most 0.000075.
Values sent between devices are 32-bit elements; how exact they have to be, the bound alone decides.
No kernel may reach another device: no remote copies, remote signals or barrier semaphores. Data moves between devices by JAX's collectives and lax.ppermute only.
A program may use at most 128 MiB of HBM per device.

```python
import jax
import jax.numpy as jnp
from jax import lax

D = 8192
TOKENS = 4096


def block_scale(own_key, shape, shards, low, top_value):
    loudness, own = 1.0, jax.random.fold_in(own_key, 6)
    for dim, parts in shards:
        heights = jnp.exp(jax.random.uniform(jax.random.fold_in(own, dim), (parts,), jnp.float32, low / len(shards), top_value / len(shards)))
        loudness = loudness * jnp.repeat(heights, shape[dim] // parts).reshape([-1 if axis == dim else 1 for axis in range(len(shape))])
    return loudness


def normal_values(key, shape, width, limit, pieces=(), kind=jnp.bfloat16):
    values = jax.random.normal(key, shape, jnp.float32) * width
    if len(pieces) > 0:
        values = block_scale(key, shape, pieces, -0.22, 0.18) * values
    return jnp.clip(values, min=-limit, max=limit).astype(kind)


def setup_inputs(seed: int = 0) -> dict:
    arg_keys = jax.random.split(jax.random.key(seed), 4)
    activations = normal_values(arg_keys[0], (TOKENS, D), (TOKENS ** -0.5), 0.09375, ((0, 2), (1, 32)), jnp.float32)
    out_grad = normal_values(arg_keys[1], (TOKENS, D), 1.0, 6.0, ((0, 64), (1, 4)), jnp.float32)
    weight = normal_values(arg_keys[2], (D, D), D ** -0.5, 0.0625, ((0, 32), (1, 4)), jnp.float32)
    return {"activations": activations, "out_grad": out_grad, "weight": weight}


def reference(activations, out_grad, weight):
    in_grad = lax.dot_general(out_grad, weight, (((1,), (1,)), ((), ())), precision=lax.Precision.HIGHEST, preferred_element_type=jnp.float32)
    weight_grad = lax.dot_general(activations, out_grad, (((0,), (0,)), ((), ())), precision=lax.Precision.HIGHEST, preferred_element_type=jnp.float32)
    return in_grad, weight_grad
```

```python
import jax
import jax.numpy as jnp
from jax import lax
from jax.sharding import PartitionSpec as P


def times_weight(grad_block, weight):
    return lax.dot_general(
        grad_block,
        weight,
        (((1,), (1,)), ((), ())),
        precision=lax.Precision.HIGH,
        preferred_element_type=jnp.float32,
    )


def outer_sum(act_block, grad_block):
    return lax.dot_general(
        act_block,
        grad_block,
        (((0,), (0,)), ((), ())),
        precision=lax.Precision.HIGH,
        preferred_element_type=jnp.float32,
    )


def local(activations, out_grad, weight):
    gathered = lax.all_gather(out_grad, "fin", axis=0, tiled=True)
    in_part = times_weight(gathered, weight)
    weight_part = outer_sum(activations, gathered)
    in_grad = lax.psum_scatter(in_part, "fout", scatter_dimension=0, tiled=True)
    weight_grad = lax.psum_scatter(weight_part, "tok", scatter_dimension=0, tiled=True)
    return (in_grad, weight_grad)


def solution(mesh):
    in_specs = (P("tok", "fin"), P(("tok", "fin"), "fout"), P("fin", "fout"))
    out_specs = (P(("tok", "fout"), "fin"), P(("fin", "tok"), "fout"))
    return jax.shard_map(local, mesh=mesh, in_specs=in_specs, out_specs=out_specs, check_vma=False)
```

```python
import functools

import jax
import jax.numpy as jnp
from jax import lax
from jax.experimental import pallas as pl
from jax.experimental.pallas import tpu as pltpu
from jax.sharding import PartitionSpec as P

AXES = ("tok", "fin", "fout")
NX, NZ = 4, 8
ROWS = 64
COLS = 1024
FEAT = 256
TILE = 256
GROUPS = ((0, 7, 1, 6, 2), (5, 3, 4))


def pairs(move):
    out = []
    for t in range(2):
        for x in range(NX):
            for z in range(NZ):
                for y in range(2):
                    for c in range(2):
                        a, b, d, e, f = move(t, x, z, y, c)
                        src = (t * NX * NZ + x * NZ + z) * 4 + 2 * y + c
                        dst = (a * NX * NZ + b * NZ + d % NZ) * 4 + 2 * e + f
                        out.append((src, dst))
    return out


ZUP = pairs(lambda t, x, z, y, c: (t, x, z + 1, y, c))
ZDOWN = pairs(lambda t, x, z, y, c: (t, x, z - 1 + NZ, y, c))
SIDE = pairs(lambda t, x, z, y, c: (t, x ^ 1, z, y, c))
MATE = pairs(lambda t, x, z, y, c: (t, x ^ 3, z, y, c))
CORE = pairs(lambda t, x, z, y, c: (t, x, z, y, 1 - c))
YLOW = pairs(lambda t, x, z, y, c: (t, x, z, 1 - y, c))
TOK = pairs(lambda t, x, z, y, c: (1 - t, x, z, y, c))
DIAG = pairs(lambda t, x, z, y, c: (1 - t, x ^ 3, z, y, c))


def send(value, perm):
    return lax.ppermute(value, AXES, perm)


def split(v):
    hi = v.astype(jnp.bfloat16)
    lo = (v - hi.astype(jnp.float32)).astype(jnp.bfloat16)
    return hi, lo


def dot(a, b, dims):
    return lax.dot_general(a, b, (dims, ((), ())), preferred_element_type=jnp.float32)


def group_body(layout, n, first, last, s_ref, *refs):
    refs = list(refs)
    take = lambda k: [refs.pop(0) for _ in range(k)]
    pieces = take(len(layout))
    own, mate = take(4 * n), take(4 * n)
    w_own, w_a, w_b = take(3)
    wg_in = None if first else take(1)[0]
    keep_ref, send_ref = take(2)
    wg_refs = take(4 if last else 1)
    ghi, glo, thi, tlo, wcat = refs
    span = n * ROWS
    spin, tok = s_ref[0], s_ref[1]
    step = pl.program_id(0)

    @pl.when(step == 0)
    def _():
        for g in range(n):
            for base, blocks in ((0, own), (FEAT, mate)):
                rows = jnp.concatenate([b[...] for b in blocks[4 * g : 4 * g + 4]], axis=0)
                hi, lo = split(rows.T)
                thi[pl.ds(base, FEAT), pl.ds(g * 256, 256)] = hi
                tlo[pl.ds(base, FEAT), pl.ds(g * 256, 256)] = lo

    for ref, parts in zip(pieces, layout):
        for start, e, k in parts:
            v = spin ^ e
            slot = (v & 1) * 2 + (v >> 1)
            hi, lo = split(ref[pl.ds(start, ROWS), :])
            rows = pl.ds(pl.multiple_of(slot * span + k * ROWS, ROWS), ROWS)
            ghi[rows, :] = hi
            glo[rows, :] = lo
    wcat[pl.ds(0, FEAT), :] = w_own[...]
    wcat[pl.ds(pl.multiple_of(FEAT + tok * 128, 128), 128), :] = w_a[...]
    wcat[pl.ds(pl.multiple_of(FEAT + (1 - tok) * 128, 128), 128), :] = w_b[...]
    whi, wlo = split(wcat[...])
    nt = ((1,), (1,))
    nn = ((1,), (0,))

    def gate(clear):
        for ref, base in ((keep_ref, 0), (send_ref, 2 * span)):
            for r in range(0, 2 * span, 128):
                rows = pl.ds(base + r, 128)
                hi = ghi[rows, :]
                term = dot(hi, whi, nt) + dot(hi, wlo, nt) + dot(glo[rows, :], whi, nt)
                if clear:
                    ref[pl.ds(r, 128), :] = term
                else:
                    ref[pl.ds(r, 128), :] += term

    pl.when(step == 0)(lambda: gate(True))
    pl.when(step > 0)(lambda: gate(False))

    for q in range(4):
        rows = pl.ds(q * 128, 128)
        acc = dot(thi[rows, :], ghi[...], nn) + dot(thi[rows, :], glo[...], nn) + dot(tlo[rows, :], ghi[...], nn)
        if not first:
            acc = acc + wg_in[rows, :]
        if not last:
            wg_refs[0][rows, :] = acc
        else:
            wcat[rows, :] = acc
    if last:
        for base, mine, other in ((0, wg_refs[0], wg_refs[1]), (FEAT, wg_refs[2], wg_refs[3])):
            mine[...] = wcat[pl.ds(pl.multiple_of(base + tok * 128, 128), 128), :]
            other[...] = wcat[pl.ds(pl.multiple_of(base + (1 - tok) * 128, 128), 128), :]


def group(index, scalars, pieces, layout, acts, a_near, a_far, weights, wg):
    turns = GROUPS[index]
    n = len(turns)
    first, last = wg is None, index == len(GROUPS) - 1
    span = n * ROWS
    tile = lambda rows: pl.BlockSpec((rows, TILE), lambda j, s: (0, j))

    def own_at(flip, r):
        return pl.BlockSpec((ROWS, FEAT), lambda j, s: ((s[2] ^ flip) * NZ + lax.rem(s[3] + r, NZ), 0))

    def mate_at(flip, r):
        return pl.BlockSpec((ROWS, FEAT), lambda j, s: ((s[4] ^ flip) * NZ + lax.rem(s[3] + r, NZ), 0))

    in_specs, args = [], []
    for v in pieces:
        in_specs.append(tile(v.shape[0]))
        args.append(v)
    for cr in range(2):
        for yr in range(2):
            for r in turns:
                in_specs.append(own_at(cr | yr << 1, r))
                args.append(acts)
    for cr in range(2):
        for yr in range(2):
            for r in turns:
                in_specs.append(mate_at(yr, r))
                args.append(a_far if cr else a_near)
    for v in weights:
        in_specs.append(tile(v.shape[0]))
        args.append(v)
    if not first:
        in_specs.append(tile(2 * FEAT))
        args.append(wg)
    whole = pl.BlockSpec((2 * span, 2 * FEAT), lambda j, s: (0, 0))
    share = jax.ShapeDtypeStruct((2 * span, 2 * FEAT), jnp.float32)
    if last:
        wg_specs = [tile(128)] * 4
        wg_shapes = [jax.ShapeDtypeStruct((128, COLS), jnp.float32)] * 4
    else:
        wg_specs = [tile(2 * FEAT)]
        wg_shapes = [jax.ShapeDtypeStruct((2 * FEAT, COLS), jnp.float32)]
    rows = 4 * span
    return pl.pallas_call(
        functools.partial(group_body, layout, n, first, last),
        grid_spec=pltpu.PrefetchScalarGridSpec(
            num_scalar_prefetch=1,
            grid=(COLS // TILE,),
            in_specs=in_specs,
            out_specs=[whole, whole, *wg_specs],
            scratch_shapes=[pltpu.VMEM((rows, TILE), jnp.bfloat16)] * 2
            + [pltpu.VMEM((2 * FEAT, rows), jnp.bfloat16)] * 2
            + [pltpu.VMEM((2 * FEAT, TILE), jnp.float32)],
        ),
        out_shape=[share, share, *wg_shapes],
        cost_estimate=pl.CostEstimate(
            flops=24 * rows * COLS * FEAT, bytes_accessed=4 * (rows * COLS + 4 * FEAT * COLS), transcendentals=0
        ),
    )(scalars, *args)


def pick(stacked, index, axis):
    return lax.dynamic_index_in_dim(stacked, index, axis, keepdims=False)


def local(acts, grad, weight):
    tok = lax.axis_index("tok")
    fin = lax.axis_index("fin")
    fout = lax.axis_index("fout")
    x, z = fin // NZ, fin % NZ
    y, c = fout // 2, fout % 2
    half = x // 2

    def side(v, which):
        return lax.dynamic_slice_in_dim(v, which * COLS, COLS, axis=1)

    m2 = send(side(grad, 1 - half), MATE)
    zs, ss, xs = {0: side(grad, half)}, {}, {}
    far = lax.dynamic_slice(weight, (tok * 128, (1 - half) * COLS), (128, COLS))
    w_a = send(far, MATE)
    w_b = send(w_a, TOK)
    w_own = side(weight, half)
    a_near = send(pick(acts.reshape(2, 2, 512, FEAT), c, 1).reshape(1024, FEAT), MATE)
    a_far = send(a_near, CORE)
    xs[0] = jnp.concatenate([m2, send(m2, SIDE)], axis=0)
    for s in range(1, 5):
        down, up = s, NZ - s
        zs[down] = send(zs[down - 1], ZDOWN)
        if s < 4:
            zs[up] = send(zs[(up + 1) % NZ], ZUP)
            xs[up] = send(xs[(up + 1) % NZ], ZUP)
            xs[down] = send(xs[down - 1], ZDOWN)
    x4 = (send(xs[5][:ROWS], ZUP), send(xs[3][ROWS:], ZDOWN))
    for r in range(NZ):
        ss[r] = send(zs[r], SIDE)

    scalars = jnp.stack([x ^ fout, tok, fout, z, y]).astype(jnp.int32)
    wg = None
    shares = {}
    for i, turns in enumerate(GROUPS):
        pieces, layout = [], []
        for k, r in enumerate(turns):
            pieces += [zs[r], ss[r]]
            layout += [((0, 0, k),), ((0, 1, k),)]
            if r == 4:
                pieces += list(x4)
                layout += [((0, 3, k),), ((0, 2, k),)]
            else:
                pieces.append(xs[r])
                layout.append(((0, 3, k), (ROWS, 2, k)))
        out = group(i, scalars, pieces, tuple(layout), acts, a_near, a_far, (w_own, w_a, w_b), wg)
        keep, give = out[:2]
        wg = out[2] if len(out) == 3 else out[2:]
        span = ROWS * len(turns)
        got = send(give, CORE)
        last = send(keep[span:] + got[span:], YLOW)
        mine = keep[:span] + got[:span] + last
        share = mine[:, :FEAT] + send(mine[:, FEAT:], MATE)
        for k, r in enumerate(turns):
            shares[r] = share[k * ROWS : (k + 1) * ROWS]

    rel = jnp.stack([shares[r] for r in range(NZ)])
    twice = jnp.concatenate([rel, rel], axis=0)
    in_grad = lax.dynamic_slice_in_dim(twice, (NZ - z) % NZ, NZ, axis=0).reshape(NZ * ROWS, FEAT)

    here = wg[0] + send(wg[1], TOK)
    there = send(wg[2], MATE) + send(wg[3], DIAG)
    weight_grad = jnp.where(half == 0, jnp.concatenate([here, there], axis=1), jnp.concatenate([there, here], axis=1))
    return (in_grad, weight_grad)


def solution(mesh):
    in_specs = (P("tok", "fin"), P(("tok", "fin"), "fout"), P("fin", "fout"))
    out_specs = (P(("tok", "fout"), "fin"), P(("fin", "tok"), "fout"))
    return jax.shard_map(local, mesh=mesh, in_specs=in_specs, out_specs=out_specs, check_vma=False)
```

```python
import functools

import jax
import jax.numpy as jnp
from jax import lax
from jax.experimental import pallas as pl
from jax.experimental.pallas import tpu as pltpu
from jax.sharding import PartitionSpec as P

AXES = ("tok", "fin", "fout")
NX, NZ = 4, 8
ROWS = 64
COLS = 1024
FEAT = 256
GROUPS = ((0, 7, 1, 6, 2), (5, 3, 4))
TILES = (256, 256)


def pairs(move):
    out = []
    for t in range(2):
        for x in range(NX):
            for z in range(NZ):
                for y in range(2):
                    for c in range(2):
                        a, b, d, e, f = move(t, x, z, y, c)
                        src = (t * NX * NZ + x * NZ + z) * 4 + 2 * y + c
                        dst = (a * NX * NZ + b * NZ + d % NZ) * 4 + 2 * e + f
                        out.append((src, dst))
    return out


ZUP = pairs(lambda t, x, z, y, c: (t, x, z + 1, y, c))
ZDOWN = pairs(lambda t, x, z, y, c: (t, x, z - 1 + NZ, y, c))
SIDE = pairs(lambda t, x, z, y, c: (t, x ^ 1, z, y, c))
MATE = pairs(lambda t, x, z, y, c: (t, x ^ 3, z, y, c))
CORE = pairs(lambda t, x, z, y, c: (t, x, z, y, 1 - c))
YLOW = pairs(lambda t, x, z, y, c: (t, x, z, 1 - y, c))
TOK = pairs(lambda t, x, z, y, c: (1 - t, x, z, y, c))
DIAG = pairs(lambda t, x, z, y, c: (1 - t, x ^ 3, z, y, c))


def send(value, perm):
    return lax.ppermute(value, AXES, perm)


def split(v):
    hi = v.astype(jnp.bfloat16)
    lo = (v - hi.astype(jnp.float32)).astype(jnp.bfloat16)
    return hi, lo


def dot(a, b, dims):
    return lax.dot_general(a, b, (dims, ((), ())), preferred_element_type=jnp.float32)


def group_body(layout, turns, tile, first, last, s_ref, *refs):
    refs = list(refs)
    take = lambda k: [refs.pop(0) for _ in range(k)]
    pieces = take(len(layout))
    a_own, a_near, a_far, w_own, w_a, w_b = take(6)
    wg_in = None if first else take(1)[0]
    keep_ref, send_ref = take(2)
    wg_refs = take(4 if last else 1)
    gl, thi, tlo, wcat = refs
    n = len(turns)
    span = n * ROWS
    spin, tok, fout, z, y = (s_ref[k] for k in range(5))
    nt = ((1,), (1,))
    nn = ((1,), (0,))

    def rows_of(ref, where, r):
        at = (where * NZ + lax.rem(z + r, NZ)) * ROWS
        return ref[pl.ds(pl.multiple_of(at, ROWS), ROWS), :]

    slots = [(cr, yr, r) for cr in range(2) for yr in range(2) for r in turns]
    for g in range(n):
        four = slots[4 * g : 4 * g + 4]
        own = [rows_of(a_own, fout ^ (cr | yr << 1), r) for cr, yr, r in four]
        mate = [rows_of(a_far if cr else a_near, y ^ yr, r) for cr, yr, r in four]
        for base, blocks in ((0, own), (FEAT, mate)):
            hi, lo = split(jnp.concatenate(blocks, axis=0).T)
            thi[pl.ds(base, FEAT), pl.ds(g * 256, 256)] = hi
            tlo[pl.ds(base, FEAT), pl.ds(g * 256, 256)] = lo

    keep_ref[...] = jnp.zeros_like(keep_ref)
    send_ref[...] = jnp.zeros_like(send_ref)
    mine = lambda base: pl.ds(pl.multiple_of(base + tok * 128, 128), 128)
    other = lambda base: pl.ds(pl.multiple_of(base + (1 - tok) * 128, 128), 128)
    high, low = pl.ds(0, tile), pl.ds(tile, tile)

    @pl.loop(0, COLS // tile)
    def _(step):
        cols = pl.ds(pl.multiple_of(step * tile, tile), tile)
        for ref, parts in zip(pieces, layout):
            for start, e, k in parts:
                v = spin ^ e
                slot = (v & 1) * 2 + (v >> 1)
                hi, lo = split(ref[pl.ds(start, ROWS), cols])
                rows = pl.ds(pl.multiple_of(slot * span + k * ROWS, ROWS), ROWS)
                gl[rows, high] = hi
                gl[rows, low] = lo
        wcat[pl.ds(0, FEAT), :] = w_own[:, cols]
        wcat[mine(FEAT), :] = w_a[:, cols]
        wcat[other(FEAT), :] = w_b[:, cols]
        whi, wlo = split(wcat[...])
        w2 = jnp.concatenate([whi, whi], axis=1)
        sums = dot(gl[...], w2, nt) + dot(gl[:, high], wlo, nt)
        keep_ref[...] += sums[: 2 * span]
        send_ref[...] += sums[2 * span :]
        acc = dot(thi[...], gl[:, high], nn) + dot(thi[...], gl[:, low], nn) + dot(tlo[...], gl[:, high], nn)
        if not first:
            acc = acc + wg_in[:, cols]
        if last:
            wcat[...] = acc
            wg_refs[0][:, cols] = wcat[mine(0), :]
            wg_refs[1][:, cols] = wcat[other(0), :]
            wg_refs[2][:, cols] = wcat[mine(FEAT), :]
            wg_refs[3][:, cols] = wcat[other(FEAT), :]
        else:
            wg_refs[0][:, cols] = acc


def group(index, scalars, pieces, layout, acts, weights, wg):
    turns, tile = GROUPS[index], TILES[index]
    first, last = wg is None, index == len(GROUPS) - 1
    span = len(turns) * ROWS
    rows = 4 * span
    args = [scalars, *pieces, *acts, *weights]
    if not first:
        args.append(wg)
    vmem = pl.BlockSpec(memory_space=pltpu.VMEM)
    share = jax.ShapeDtypeStruct((2 * span, 2 * FEAT), jnp.float32)
    if last:
        grads = [jax.ShapeDtypeStruct((128, COLS), jnp.float32)] * 4
    else:
        grads = [jax.ShapeDtypeStruct((2 * FEAT, COLS), jnp.float32)]
    return pl.pallas_call(
        functools.partial(group_body, layout, turns, tile, first, last),
        in_specs=[pl.BlockSpec(memory_space=pltpu.SMEM)] + [vmem] * (len(args) - 1),
        out_specs=[vmem] * (2 + len(grads)),
        out_shape=[share, share, *grads],
        scratch_shapes=[pltpu.VMEM((rows, 2 * tile), jnp.bfloat16)]
        + [pltpu.VMEM((2 * FEAT, rows), jnp.bfloat16)] * 2
        + [pltpu.VMEM((2 * FEAT, tile), jnp.float32)],
        input_output_aliases={} if first or last else {len(args) - 1: 2},
        compiler_params=pltpu.CompilerParams(vmem_limit_bytes=20 << 20),
        cost_estimate=pl.CostEstimate(
            flops=24 * rows * COLS * FEAT, bytes_accessed=4 * (rows * COLS + 4 * FEAT * COLS), transcendentals=0
        ),
    )(*args)


def pick(stacked, index, axis):
    return lax.dynamic_index_in_dim(stacked, index, axis, keepdims=False)


def local(acts, grad, weight):
    tok = lax.axis_index("tok")
    fin = lax.axis_index("fin")
    fout = lax.axis_index("fout")
    x, z = fin // NZ, fin % NZ
    y, c = fout // 2, fout % 2
    half = x // 2

    def side(v, which):
        return lax.dynamic_slice_in_dim(v, which * COLS, COLS, axis=1)

    m2 = send(side(grad, 1 - half), MATE)
    zs, ss, xs = {0: side(grad, half)}, {}, {}
    far = lax.dynamic_slice(weight, (tok * 128, (1 - half) * COLS), (128, COLS))
    w_a = send(far, MATE)
    w_b = send(w_a, TOK)
    w_own = side(weight, half)
    a_near = send(pick(acts.reshape(2, 2, 512, FEAT), c, 1).reshape(1024, FEAT), MATE)
    a_far = send(a_near, CORE)
    xs[0] = jnp.concatenate([m2, send(m2, SIDE)], axis=0)
    for s in range(1, 5):
        down, up = s, NZ - s
        zs[down] = send(zs[down - 1], ZDOWN)
        if s < 4:
            zs[up] = send(zs[(up + 1) % NZ], ZUP)
            xs[up] = send(xs[(up + 1) % NZ], ZUP)
            xs[down] = send(xs[down - 1], ZDOWN)
    for r in range(NZ):
        ss[r] = send(zs[r], SIDE)

    scalars = jnp.stack([x ^ fout, tok, fout, z, y]).astype(jnp.int32)
    wg = None
    shares = []
    for i, turns in enumerate(GROUPS):
        pieces, layout = [], []
        if i == 1:
            x5, x3, wg = lax.optimization_barrier((xs[5], xs[3], wg))
            x4 = (send(x5[:ROWS], ZUP), send(x3[ROWS:], ZDOWN))
        for k, r in enumerate(turns):
            pieces += [zs[r], ss[r]]
            layout += [((0, 0, k),), ((0, 1, k),)]
            if r == 4:
                pieces += list(x4)
                layout += [((0, 3, k),), ((0, 2, k),)]
            else:
                pieces.append(xs[r])
                layout.append(((0, 3, k), (ROWS, 2, k)))
        out = group(i, scalars, pieces, tuple(layout), (acts, a_near, a_far), (w_own, w_a, w_b), wg)
        keep, give = out[:2]
        wg = out[2] if len(out) == 3 else out[2:]
        span = ROWS * len(turns)
        got = send(give, CORE)
        both = keep[:, :FEAT] + got[:, :FEAT] + send(keep[:, FEAT:] + got[:, FEAT:], MATE)
        shares.append((both[:span], send(both[span:], YLOW)))

    far = [send(wg[1], TOK), send(wg[2], MATE), send(wg[3], DIAG)]
    far, last = lax.optimization_barrier((far, [v[1] for v in shares]))
    parts = {}
    for turns, (mine, _), other in zip(GROUPS, shares, last):
        total = mine + other
        for k, r in enumerate(turns):
            parts[r] = total[k * ROWS : (k + 1) * ROWS]
    rel = jnp.stack([parts[r] for r in range(NZ)])
    twice = jnp.concatenate([rel, rel], axis=0)
    in_grad = lax.dynamic_slice_in_dim(twice, (NZ - z) % NZ, NZ, axis=0).reshape(NZ * ROWS, FEAT)
    here, there = wg[0] + far[0], far[1] + far[2]
    weight_grad = jnp.where(half == 0, jnp.concatenate([here, there], axis=1), jnp.concatenate([there, here], axis=1))
    return (in_grad, weight_grad)


def solution(mesh):
    in_specs = (P("tok", "fin"), P(("tok", "fin"), "fout"), P("fin", "fout"))
    out_specs = (P(("tok", "fout"), "fin"), P(("fin", "tok"), "fout"))
    return jax.shard_map(local, mesh=mesh, in_specs=in_specs, out_specs=out_specs, check_vma=False)
```

```python
import functools

import jax
import jax.numpy as jnp
from jax import lax
from jax.experimental import pallas as pl
from jax.experimental.pallas import tpu as pltpu
from jax.sharding import PartitionSpec as P

AXES = ("tok", "fin", "fout")
NX, NZ = 4, 8
ROWS = 64
COLS = 1024
FEAT = 256
GROUPS = ((0, 7, 1, 6, 2), (5, 3, 4))
TILES = (256, 256)


def pairs(move):
    out = []
    for t in range(2):
        for x in range(NX):
            for z in range(NZ):
                for y in range(2):
                    for c in range(2):
                        a, b, d, e, f = move(t, x, z, y, c)
                        src = (t * NX * NZ + x * NZ + z) * 4 + 2 * y + c
                        dst = (a * NX * NZ + b * NZ + d % NZ) * 4 + 2 * e + f
                        out.append((src, dst))
    return out


ZUP = pairs(lambda t, x, z, y, c: (t, x, z + 1, y, c))
ZDOWN = pairs(lambda t, x, z, y, c: (t, x, z - 1 + NZ, y, c))
SIDE = pairs(lambda t, x, z, y, c: (t, x ^ 1, z, y, c))
MATE = pairs(lambda t, x, z, y, c: (t, x ^ 3, z, y, c))
CORE = pairs(lambda t, x, z, y, c: (t, x, z, y, 1 - c))
YLOW = pairs(lambda t, x, z, y, c: (t, x, z, 1 - y, c))
TOK = pairs(lambda t, x, z, y, c: (1 - t, x, z, y, c))
DIAG = pairs(lambda t, x, z, y, c: (1 - t, x ^ 3, z, y, c))


def send(value, perm):
    return lax.ppermute(value, AXES, perm)


def split(v):
    hi = v.astype(jnp.bfloat16)
    lo = (v - hi.astype(jnp.float32)).astype(jnp.bfloat16)
    return hi, lo


def dot(a, b, dims):
    return lax.dot_general(a, b, (dims, ((), ())), preferred_element_type=jnp.float32)


def group_body(layout, turns, tile, first, last, s_ref, *refs):
    refs = list(refs)
    take = lambda k: [refs.pop(0) for _ in range(k)]
    pieces = take(len(layout))
    a_own, a_near, a_far, w_own, w_a, w_b = take(6)
    wg_in = None if first else take(1)[0]
    keep_ref, send_ref = take(2)
    wg_refs = take(4 if last else 1)
    bufs, (thi, tlo) = (refs[:2], refs[2:4]), refs[4:]
    n = len(turns)
    span = n * ROWS
    spin, tok, fout, z, y = (s_ref[k] for k in range(5))
    nt = ((1,), (1,))
    nn = ((1,), (0,))

    def rows_of(ref, where, r):
        at = (where * NZ + lax.rem(z + r, NZ)) * ROWS
        return ref[pl.ds(pl.multiple_of(at, ROWS), ROWS), :]

    slots = [(cr, yr, r) for cr in range(2) for yr in range(2) for r in turns]
    for g in range(n):
        four = slots[4 * g : 4 * g + 4]
        own = [rows_of(a_own, fout ^ (cr | yr << 1), r) for cr, yr, r in four]
        mate = [rows_of(a_far if cr else a_near, y ^ yr, r) for cr, yr, r in four]
        for base, blocks in ((0, own), (FEAT, mate)):
            hi, lo = split(jnp.concatenate(blocks, axis=0).T)
            thi[pl.ds(base, FEAT), pl.ds(g * 256, 256)] = hi
            tlo[pl.ds(base, FEAT), pl.ds(g * 256, 256)] = lo

    keep_ref[...] = jnp.zeros_like(keep_ref)
    send_ref[...] = jnp.zeros_like(send_ref)
    mine = lambda base: pl.ds(pl.multiple_of(base + tok * 128, 128), 128)
    other = lambda base: pl.ds(pl.multiple_of(base + (1 - tok) * 128, 128), 128)
    high, low = pl.ds(0, tile), pl.ds(tile, tile)

    def tile_at(step, gl, wcat):
        cols = pl.ds(pl.multiple_of(step * tile, tile), tile)
        for ref, parts in zip(pieces, layout):
            for start, e, k in parts:
                v = spin ^ e
                slot = (v & 1) * 2 + (v >> 1)
                hi, lo = split(ref[pl.ds(start, ROWS), cols])
                rows = pl.ds(pl.multiple_of(slot * span + k * ROWS, ROWS), ROWS)
                gl[rows, high] = hi
                gl[rows, low] = lo
        wcat[pl.ds(0, FEAT), :] = w_own[:, cols]
        wcat[mine(FEAT), :] = w_a[:, cols]
        wcat[other(FEAT), :] = w_b[:, cols]
        whi, wlo = split(wcat[...])
        w2 = jnp.concatenate([whi, whi], axis=1)
        sums = dot(gl[...], w2, nt) + dot(gl[:, high], wlo, nt)
        keep_ref[...] += sums[: 2 * span]
        send_ref[...] += sums[2 * span :]
        acc = dot(thi[...], gl[:, high], nn) + dot(thi[...], gl[:, low], nn) + dot(tlo[...], gl[:, high], nn)
        if not first:
            acc = acc + wg_in[:, cols]
        if last:
            wcat[...] = acc
            wg_refs[0][:, cols] = wcat[mine(0), :]
            wg_refs[1][:, cols] = wcat[other(0), :]
            wg_refs[2][:, cols] = wcat[mine(FEAT), :]
            wg_refs[3][:, cols] = wcat[other(FEAT), :]
        else:
            wg_refs[0][:, cols] = acc

    @pl.loop(0, COLS // tile // 2)
    def _(pair):
        for k in range(2):
            tile_at(2 * pair + k, bufs[0][k], bufs[1][k])


def group(index, scalars, pieces, layout, acts, weights, wg):
    turns, tile = GROUPS[index], TILES[index]
    first, last = wg is None, index == len(GROUPS) - 1
    span = len(turns) * ROWS
    rows = 4 * span
    args = [scalars, *pieces, *acts, *weights]
    if not first:
        args.append(wg)
    vmem = pl.BlockSpec(memory_space=pltpu.VMEM)
    share = jax.ShapeDtypeStruct((2 * span, 2 * FEAT), jnp.float32)
    if last:
        grads = [jax.ShapeDtypeStruct((128, COLS), jnp.float32)] * 4
    else:
        grads = [jax.ShapeDtypeStruct((2 * FEAT, COLS), jnp.float32)]
    return pl.pallas_call(
        functools.partial(group_body, layout, turns, tile, first, last),
        in_specs=[pl.BlockSpec(memory_space=pltpu.SMEM)] + [vmem] * (len(args) - 1),
        out_specs=[vmem] * (2 + len(grads)),
        out_shape=[share, share, *grads],
        scratch_shapes=[pltpu.VMEM((rows, 2 * tile), jnp.bfloat16)] * 2
        + [pltpu.VMEM((2 * FEAT, tile), jnp.float32)] * 2
        + [pltpu.VMEM((2 * FEAT, rows), jnp.bfloat16)] * 2,
        input_output_aliases={} if first or last else {len(args) - 1: 2},
        compiler_params=pltpu.CompilerParams(vmem_limit_bytes=20 << 20),
        cost_estimate=pl.CostEstimate(
            flops=24 * rows * COLS * FEAT, bytes_accessed=4 * (rows * COLS + 4 * FEAT * COLS), transcendentals=0
        ),
    )(*args)


def finish_body(s_ref, *refs):
    shares, grads, (in_ref, wg_ref) = refs[:4], refs[4:8], refs[8:]
    z, half = s_ref[3], s_ref[5]
    for g, turns in enumerate(GROUPS):
        for k, r in enumerate(turns):
            at = pl.multiple_of(lax.rem(z + r, NZ) * ROWS, ROWS)
            rows = pl.ds(k * ROWS, ROWS)
            in_ref[pl.ds(at, ROWS), :] = shares[2 * g][rows, :] + shares[2 * g + 1][rows, :]
    here = pl.ds(pl.multiple_of(half * COLS, COLS), COLS)
    there = pl.ds(pl.multiple_of((1 - half) * COLS, COLS), COLS)
    wg_ref[:, here] = grads[0][...] + grads[1][...]
    wg_ref[:, there] = grads[2][...] + grads[3][...]


def finish(scalars, shares, grads):
    vmem = pl.BlockSpec(memory_space=pltpu.VMEM)
    return pl.pallas_call(
        finish_body,
        in_specs=[pl.BlockSpec(memory_space=pltpu.SMEM)] + [vmem] * 8,
        out_shape=[
            jax.ShapeDtypeStruct((NZ * ROWS, FEAT), jnp.float32),
            jax.ShapeDtypeStruct((FEAT // 2, 2 * COLS), jnp.float32),
        ],
        compiler_params=pltpu.CompilerParams(vmem_limit_bytes=16 << 20),
        cost_estimate=pl.CostEstimate(flops=1 << 20, bytes_accessed=4 << 20, transcendentals=0),
    )(scalars, *shares, *grads)


def pick(stacked, index, axis):
    return lax.dynamic_index_in_dim(stacked, index, axis, keepdims=False)


def local(acts, grad, weight):
    tok = lax.axis_index("tok")
    fin = lax.axis_index("fin")
    fout = lax.axis_index("fout")
    x, z = fin // NZ, fin % NZ
    y, c = fout // 2, fout % 2
    half = x // 2

    def side(v, which):
        return lax.dynamic_slice_in_dim(v, which * COLS, COLS, axis=1)

    m2 = send(side(grad, 1 - half), MATE)
    zs, ss, xs = {0: side(grad, half)}, {}, {}
    far = lax.dynamic_slice(weight, (tok * 128, (1 - half) * COLS), (128, COLS))
    w_a = send(far, MATE)
    w_b = send(w_a, TOK)
    w_own = side(weight, half)
    a_near = send(pick(acts.reshape(2, 2, 512, FEAT), c, 1).reshape(1024, FEAT), MATE)
    a_far = send(a_near, CORE)
    xs[0] = jnp.concatenate([m2, send(m2, SIDE)], axis=0)
    for s in range(1, 5):
        down, up = s, NZ - s
        zs[down] = send(zs[down - 1], ZDOWN)
        if s < 4:
            zs[up] = send(zs[(up + 1) % NZ], ZUP)
            xs[up] = send(xs[(up + 1) % NZ], ZUP)
            xs[down] = send(xs[down - 1], ZDOWN)
    for r in range(NZ):
        ss[r] = send(zs[r], SIDE)

    scalars = jnp.stack([x ^ fout, tok, fout, z, y, half]).astype(jnp.int32)
    wg = None
    shares = []
    for i, turns in enumerate(GROUPS):
        pieces, layout = [], []
        if i == 1:
            x5, x3, wg = lax.optimization_barrier((xs[5], xs[3], wg))
            x4 = (send(x5[:ROWS], ZUP), send(x3[ROWS:], ZDOWN))
        for k, r in enumerate(turns):
            pieces += [zs[r], ss[r]]
            layout += [((0, 0, k),), ((0, 1, k),)]
            if r == 4:
                pieces += list(x4)
                layout += [((0, 3, k),), ((0, 2, k),)]
            else:
                pieces.append(xs[r])
                layout.append(((0, 3, k), (ROWS, 2, k)))
        out = group(i, scalars, pieces, tuple(layout), (acts, a_near, a_far), (w_own, w_a, w_b), wg)
        keep, give = out[:2]
        wg = out[2] if len(out) == 3 else out[2:]
        span = ROWS * len(turns)
        got = send(give, CORE)
        mine = keep[:span] + got[:span] + send(keep[span:] + got[span:], YLOW)
        shares += [mine[:, :FEAT], send(mine[:, FEAT:], MATE)]

    far = (send(wg[1], TOK), send(wg[2], MATE), send(wg[3], DIAG))
    return finish(scalars, shares, (wg[0], *far))


def solution(mesh):
    in_specs = (P("tok", "fin"), P(("tok", "fin"), "fout"), P("fin", "fout"))
    out_specs = (P(("tok", "fout"), "fin"), P(("fin", "tok"), "fout"))
    return jax.shard_map(local, mesh=mesh, in_specs=in_specs, out_specs=out_specs, check_vma=False)
```

```python
import functools

import jax
import jax.numpy as jnp
from jax import lax
from jax.experimental import pallas as pl
from jax.experimental.pallas import tpu as pltpu
from jax.sharding import PartitionSpec as P

AXES = ("tok", "fin", "fout")
NX, NZ = 4, 8
ROWS = 64
COLS = 1024
FEAT = 256
GROUPS = ((0, 7, 1, 6, 2), (5, 3), (5, 3, 4))
BATCHES = ((0, 7, 1, 6, 2), (5, 3), (4,))
TILES = (256, 256, 512)


def pairs(move):
    out = []
    for t in range(2):
        for x in range(NX):
            for z in range(NZ):
                for y in range(2):
                    for c in range(2):
                        a, b, d, e, f = move(t, x, z, y, c)
                        src = (t * NX * NZ + x * NZ + z) * 4 + 2 * y + c
                        dst = (a * NX * NZ + b * NZ + d % NZ) * 4 + 2 * e + f
                        out.append((src, dst))
    return out


ZUP = pairs(lambda t, x, z, y, c: (t, x, z + 1, y, c))
ZDOWN = pairs(lambda t, x, z, y, c: (t, x, z - 1 + NZ, y, c))
SIDE = pairs(lambda t, x, z, y, c: (t, x ^ 1, z, y, c))
MATE = pairs(lambda t, x, z, y, c: (t, x ^ 3, z, y, c))
CORE = pairs(lambda t, x, z, y, c: (t, x, z, y, 1 - c))
YLOW = pairs(lambda t, x, z, y, c: (t, x, z, 1 - y, c))
TOK = pairs(lambda t, x, z, y, c: (1 - t, x, z, y, c))


def send(value, perm):
    return lax.ppermute(value, AXES, perm)


def split(v):
    hi = v.astype(jnp.bfloat16)
    lo = (v - hi.astype(jnp.float32)).astype(jnp.bfloat16)
    return hi, lo


def dot(a, b, dims):
    return lax.dot_general(a, b, (dims, ((), ())), preferred_element_type=jnp.float32)


def group_body(layout, turns, tile, emit, outer, first, last, s_ref, *refs):
    refs = list(refs)
    take = lambda k: [refs.pop(0) for _ in range(k)]
    pieces = take(len(layout))
    a_own, a_near, a_far = take(3) if outer else (None,) * 3
    w_own, w_a, w_b = take(3)
    wg_in = take(1)[0] if outer and not first else None
    keep_ref, send_ref = take(2)
    wg_refs = take((4 if last else 1) if outer else 0)
    bufs = (refs[:2], refs[2:4])
    thi, tlo = refs[4:] if outer else (None, None)
    n = len(turns)
    span = n * ROWS
    spin, tok, fout, z, y = (s_ref[k] for k in range(5))
    nt = ((1,), (1,))
    nn = ((1,), (0,))

    def rows_of(ref, where, r):
        at = (where * NZ + lax.rem(z + r, NZ)) * ROWS
        return ref[pl.ds(pl.multiple_of(at, ROWS), ROWS), :]

    slots = [(cr, yr, r) for cr in range(2) for yr in range(2) for r in turns]
    for g in range(n if outer else 0):
        four = slots[4 * g : 4 * g + 4]
        own = [rows_of(a_own, fout ^ (cr | yr << 1), r) for cr, yr, r in four]
        mate = [rows_of(a_far if cr else a_near, y ^ yr, r) for cr, yr, r in four]
        for base, blocks in ((0, own), (FEAT, mate)):
            hi, lo = split(jnp.concatenate(blocks, axis=0).T)
            thi[pl.ds(base, FEAT), pl.ds(g * 256, 256)] = hi
            tlo[pl.ds(base, FEAT), pl.ds(g * 256, 256)] = lo

    keep_ref[...] = jnp.zeros_like(keep_ref)
    send_ref[...] = jnp.zeros_like(send_ref)
    mine = lambda base: pl.ds(pl.multiple_of(base + tok * 128, 128), 128)
    other = lambda base: pl.ds(pl.multiple_of(base + (1 - tok) * 128, 128), 128)
    high, low = pl.ds(0, tile), pl.ds(tile, tile)

    def tile_at(step, gl, wcat):
        cols = pl.ds(pl.multiple_of(step * tile, tile), tile)
        for ref, parts in zip(pieces, layout):
            for start, e, k in parts:
                v = spin ^ e
                slot = (v & 1) * 2 + (v >> 1)
                hi, lo = split(ref[pl.ds(start, ROWS), cols])
                rows = pl.ds(pl.multiple_of(slot * span + k * ROWS, ROWS), ROWS)
                gl[rows, high] = hi
                gl[rows, low] = lo
        wcat[pl.ds(0, FEAT), :] = w_own[:, cols]
        wcat[mine(FEAT), :] = w_a[:, cols]
        wcat[other(FEAT), :] = w_b[:, cols]
        whi, wlo = split(wcat[...])
        w2 = jnp.concatenate([whi, whi], axis=1)
        if len(emit) == n:
            rows = gl[...]
        else:
            rows = jnp.concatenate([gl[pl.ds(q * span + k * ROWS, ROWS), :] for q in range(4) for k in emit], axis=0)
        sums = dot(rows, w2, nt) + dot(rows[:, :tile], wlo, nt)
        keep_ref[...] += sums[: 2 * len(emit) * ROWS]
        send_ref[...] += sums[2 * len(emit) * ROWS :]
        if not outer:
            return
        acc = dot(thi[...], gl[:, high], nn) + dot(thi[...], gl[:, low], nn) + dot(tlo[...], gl[:, high], nn)
        if not first:
            acc = acc + wg_in[:, cols]
        if last:
            wcat[...] = acc
            wg_refs[0][:, cols] = wcat[mine(0), :]
            wg_refs[1][:, cols] = wcat[other(0), :]
            wg_refs[2][:, cols] = wcat[mine(FEAT), :]
            wg_refs[3][:, cols] = wcat[other(FEAT), :]
        else:
            wg_refs[0][:, cols] = acc

    @pl.loop(0, COLS // tile // 2)
    def _(pair):
        for k in range(2):
            tile_at(2 * pair + k, bufs[0][k], bufs[1][k])


def group(index, scalars, pieces, layout, acts, weights, wg):
    turns, tile = GROUPS[index], TILES[index]
    emit = tuple(k for k, r in enumerate(turns) if r in BATCHES[index])
    outer, first, last = index != 1, wg is None, index == len(GROUPS) - 1
    rows = 4 * len(turns) * ROWS
    args = [scalars, *pieces, *(acts if outer else ()), *weights]
    if outer and not first:
        args.append(wg)
    vmem = pl.BlockSpec(memory_space=pltpu.VMEM)
    share = jax.ShapeDtypeStruct((2 * len(emit) * ROWS, 2 * FEAT), jnp.float32)
    grads = []
    if outer and last:
        grads = [jax.ShapeDtypeStruct((128, COLS), jnp.float32)] * 4
    elif outer:
        grads = [jax.ShapeDtypeStruct((2 * FEAT, COLS), jnp.float32)]
    scratch = [pltpu.VMEM((rows, 2 * tile), jnp.bfloat16)] * 2 + [pltpu.VMEM((2 * FEAT, tile), jnp.float32)] * 2
    if outer:
        scratch += [pltpu.VMEM((2 * FEAT, rows), jnp.bfloat16)] * 2
    return pl.pallas_call(
        functools.partial(group_body, layout, turns, tile, emit, outer, first, last),
        in_specs=[pl.BlockSpec(memory_space=pltpu.SMEM)] + [vmem] * (len(args) - 1),
        out_specs=[vmem] * (2 + len(grads)),
        out_shape=[share, share, *grads],
        scratch_shapes=scratch,
        compiler_params=pltpu.CompilerParams(vmem_limit_bytes=20 << 20),
        cost_estimate=pl.CostEstimate(
            flops=24 * rows * COLS * FEAT, bytes_accessed=4 * (rows * COLS + 4 * FEAT * COLS), transcendentals=0
        ),
    )(*args)


def finish_body(s_ref, *refs):
    shares, grads, (in_ref, wg_ref) = refs[:6], refs[6:9], refs[9:]
    z, half = s_ref[3], s_ref[5]
    for g, turns in enumerate(BATCHES):
        for k, r in enumerate(turns):
            at = pl.multiple_of(lax.rem(z + r, NZ) * ROWS, ROWS)
            rows = pl.ds(k * ROWS, ROWS)
            in_ref[pl.ds(at, ROWS), :] = shares[2 * g][rows, :] + shares[2 * g + 1][rows, :]
    here = pl.ds(pl.multiple_of(half * COLS, COLS), COLS)
    there = pl.ds(pl.multiple_of((1 - half) * COLS, COLS), COLS)
    wg_ref[:, here] = grads[0][...] + grads[1][...]
    wg_ref[:, there] = grads[2][...]


def finish(scalars, shares, grads):
    vmem = pl.BlockSpec(memory_space=pltpu.VMEM)
    return pl.pallas_call(
        finish_body,
        in_specs=[pl.BlockSpec(memory_space=pltpu.SMEM)] + [vmem] * 9,
        out_shape=[
            jax.ShapeDtypeStruct((NZ * ROWS, FEAT), jnp.float32),
            jax.ShapeDtypeStruct((FEAT // 2, 2 * COLS), jnp.float32),
        ],
        compiler_params=pltpu.CompilerParams(vmem_limit_bytes=16 << 20),
        cost_estimate=pl.CostEstimate(flops=1 << 20, bytes_accessed=4 << 20, transcendentals=0),
    )(scalars, *shares, *grads)


def pick(stacked, index, axis):
    return lax.dynamic_index_in_dim(stacked, index, axis, keepdims=False)


def local(acts, grad, weight):
    tok = lax.axis_index("tok")
    fin = lax.axis_index("fin")
    fout = lax.axis_index("fout")
    x, z = fin // NZ, fin % NZ
    y, c = fout // 2, fout % 2
    half = x // 2

    def side(v, which):
        return lax.dynamic_slice_in_dim(v, which * COLS, COLS, axis=1)

    m2 = send(side(grad, 1 - half), MATE)
    zs, ss, xs = {0: side(grad, half)}, {}, {}
    far = lax.dynamic_slice(weight, (tok * 128, (1 - half) * COLS), (128, COLS))
    w_a = send(far, MATE)
    w_b = send(w_a, TOK)
    w_own = side(weight, half)
    a_near = send(pick(acts.reshape(2, 2, 512, FEAT), c, 1).reshape(1024, FEAT), MATE)
    a_far = send(a_near, CORE)
    xs[0] = jnp.concatenate([m2, send(m2, SIDE)], axis=0)
    for s in range(1, 5):
        down, up = s, NZ - s
        zs[down] = send(zs[down - 1], ZDOWN)
        if s < 4:
            zs[up] = send(zs[(up + 1) % NZ], ZUP)
            xs[up] = send(xs[(up + 1) % NZ], ZUP)
            xs[down] = send(xs[down - 1], ZDOWN)
    for r in range(NZ):
        ss[r] = send(zs[r], SIDE)

    scalars = jnp.stack([x ^ fout, tok, fout, z, y, half]).astype(jnp.int32)
    wg = None
    shares = []
    for i, turns in enumerate(GROUPS):
        pieces, layout = [], []
        if i == 1:
            x5, x3, wg = lax.optimization_barrier((xs[5], xs[3], wg))
            x4 = (send(x5[:ROWS], ZUP), send(x3[ROWS:], ZDOWN))
        for k, r in enumerate(turns):
            pieces += [zs[r], ss[r]]
            layout += [((0, 0, k),), ((0, 1, k),)]
            if r == 4:
                pieces += list(x4)
                layout += [((0, 3, k),), ((0, 2, k),)]
            else:
                pieces.append(xs[r])
                layout.append(((0, 3, k), (ROWS, 2, k)))
        out = group(i, scalars, pieces, tuple(layout), (acts, a_near, a_far), (w_own, w_a, w_b), wg)
        keep, give = out[:2]
        if i != 1:
            wg = out[2] if len(out) == 3 else out[2:]
        span = ROWS * len(BATCHES[i])
        got = send(give, CORE)
        if i == 0:
            other = send(keep[span:] + got[span:], YLOW)
            mine = keep[:span] + got[:span] + other
            give = mine[:, FEAT:]
            shares += [mine[:, :FEAT], send(give, MATE)]
        else:
            give = keep[:, FEAT:] + got[:, FEAT:]
            both = keep[:, :FEAT] + got[:, :FEAT] + send(give, MATE)
            shares += [both[:span], send(both[span:], YLOW)]

    there = send(wg[2] + send(wg[3], TOK), MATE)
    far = (send(wg[1], TOK), there)
    return finish(scalars, shares, (wg[0], *far))


def solution(mesh):
    in_specs = (P("tok", "fin"), P(("tok", "fin"), "fout"), P("fin", "fout"))
    out_specs = (P(("tok", "fout"), "fin"), P(("fin", "tok"), "fout"))
    return jax.shard_map(local, mesh=mesh, in_specs=in_specs, out_specs=out_specs, check_vma=False)
```
